128 devices in a mesh: rows: 16 (over y, z_lo, core), cols: 8 (over x, z_hi).
Axes of the slice: x: 4, y: 4, z: 4 (z_hi: 2, z_lo: 2; z = z_hi * 2 + z_lo), core: 2. Of those that a mesh axis runs over, the one named last changes fastest.
Arguments:
- features: bfloat16 [512, 1024, 192], P('rows', 'cols'), may hold values from -6 to 6
- gain_conv: float32 [192], replicated, may hold values from 0.1 to 1.9
- w_expand: bfloat16 [192, 768], replicated, may hold values from -0.4375 to 0.4375
- w_depth: bfloat16 [3, 3, 768], replicated, may hold values from -2 to 2
- w_project: bfloat16 [768, 192], replicated, may hold values from -0.21875 to 0.21875
- gain_block: float32 [192], replicated, may hold values from 0.1 to 1.9
- qkv_block: bfloat16 [192, 576], replicated, may hold values from -18 to 18, as said below
- out_block: bfloat16 [192, 192], replicated, may hold values from -0.4375 to 0.4375
- gain_bffn: float32 [192], replicated, may hold values from 0.1 to 1.9
- ffn_in_block: bfloat16 [192, 768], replicated, may hold values from -0.4375 to 0.4375
- ffn_out_block: bfloat16 [768, 192], replicated, may hold values from -0.21875 to 0.21875
- gain_grid: float32 [192], replicated, may hold values from 0.1 to 1.9
- qkv_grid: bfloat16 [192, 576], replicated, may hold values from -18 to 18, as said below
- out_grid: bfloat16 [192, 192], replicated, may hold values from -0.4375 to 0.4375
- gain_gffn: float32 [192], replicated, may hold values from 0.1 to 1.9
- ffn_in_grid: bfloat16 [192, 768], replicated, may hold values from -0.4375 to 0.4375
- ffn_out_grid: bfloat16 [768, 192], replicated, may hold values from -0.21875 to 0.21875
Outputs:
- result: bfloat16 [512, 1024, 192], P('rows', 'cols')
The draws below stay inside these ranges and needn't reach their ends.
Inputs may be any that keep to these rules, and one draw needn't show every extreme that they name: `qkv_block`: columns hold the queries, keys and values, each grouped by head. `qkv_grid`: columns hold the queries, keys and values, each grouped by head.
All inputs are finite; a program needn't handle non-finite values.
Results may differ from the reference program's by a relative error of at most 0.023.
Values may be sent and summed in bfloat16 or wider, within the bound.
A program may use at most 128 MiB of HBM per device.

```python
import jax
import jax.numpy as jnp
from jax import lax

C = 192
HID = 768
HEADS = 6
BLOCK = 8
G = 16
H = 512
W = 1024
STRIDE_R = 32
STRIDE_C = 64


def projection_law(key):
    first_key = jax.random.fold_in(key, 0)
    base = jnp.clip(jax.random.normal(first_key, (C, 3 * C), jnp.float32), -4.0, 4.0) * C ** (-0.5)
    return base


def draw_qkv_block(key, part):
    return projection_law(jax.random.fold_in(key, 11)).astype(jnp.bfloat16)


def draw_qkv_grid(key, part):
    return projection_law(jax.random.fold_in(key, 29)).astype(jnp.bfloat16)


def steps_of(rng, extent, pieces, least, top_value):
    level = 1.0
    for dim, blocks in pieces:
        steps = jax.random.uniform(jax.random.fold_in(jax.random.fold_in(rng, 6), dim), (blocks,), jnp.float32, least / len(pieces), top_value / len(pieces))
        level = level * jnp.repeat(jnp.exp(steps), extent[dim] // blocks).reshape((-1,) + (1,) * (len(extent) - 1 - dim))
    return level


def bell_draw(key, extent, spread, bound, cuts=(), held_as=jnp.bfloat16):
    entries = spread * jax.random.normal(key, extent, jnp.float32)
    if cuts:
        entries = entries * steps_of(key, extent, cuts, -0.22, 0.18)
    return jnp.clip(entries, -bound, bound).astype(held_as)


def setup_inputs(seed: int = 0) -> dict:
    arg_keys = jax.random.split(jax.random.key(seed), 18)
    features = bell_draw(arg_keys[0], (H, W, C), 1.0, 6.0, ((0, 16), (1, 8)))
    gain_conv = jnp.clip(1.0 + 0.18 * jax.random.normal(arg_keys[1], (C,), jnp.float32), 0.1, 1.9)
    w_expand = bell_draw(arg_keys[2], (C, HID), C ** -0.5, 0.4375)
    w_depth = bell_draw(arg_keys[3], (3, 3, HID), 9 ** -0.5, 2.0)
    w_project = bell_draw(arg_keys[4], (HID, C), HID ** -0.5, 0.21875)
    gain_block = jnp.clip(1.0 + 0.18 * jax.random.normal(arg_keys[5], (C,), jnp.float32), 0.1, 1.9)
    qkv_block = draw_qkv_block(jax.random.fold_in(arg_keys[17], 71), 0)
    out_block = bell_draw(arg_keys[7], (C, C), C ** -0.5, 0.4375)
    gain_bffn = jnp.clip(1.0 + 0.18 * jax.random.normal(arg_keys[8], (C,), jnp.float32), 0.1, 1.9)
    ffn_in_block = bell_draw(arg_keys[9], (C, HID), C ** -0.5, 0.4375)
    ffn_out_block = bell_draw(arg_keys[10], (HID, C), HID ** -0.5, 0.21875)
    gain_grid = jnp.clip(1.0 + 0.18 * jax.random.normal(arg_keys[11], (C,), jnp.float32), 0.1, 1.9)
    qkv_grid = draw_qkv_grid(jax.random.fold_in(arg_keys[17], 71), 0)
    out_grid = bell_draw(arg_keys[13], (C, C), C ** -0.5, 0.4375)
    gain_gffn = jnp.clip(1.0 + 0.18 * jax.random.normal(arg_keys[14], (C,), jnp.float32), 0.1, 1.9)
    ffn_in_grid = bell_draw(arg_keys[15], (C, HID), C ** -0.5, 0.4375)
    ffn_out_grid = bell_draw(arg_keys[16], (HID, C), HID ** -0.5, 0.21875)
    return dict(features=features, gain_conv=gain_conv, w_expand=w_expand, w_depth=w_depth, w_project=w_project, gain_block=gain_block, qkv_block=qkv_block, out_block=out_block, gain_bffn=gain_bffn, ffn_in_block=ffn_in_block, ffn_out_block=ffn_out_block, gain_grid=gain_grid, qkv_grid=qkv_grid, out_grid=out_grid, gain_gffn=gain_gffn, ffn_in_grid=ffn_in_grid, ffn_out_grid=ffn_out_grid)


EPSILON = 1e-05

def layer_norm(values, scale_gain):
    values = values.astype(jnp.float32)
    average = lax.optimization_barrier(jnp.mean(values, axis=-1, keepdims=True))
    centred = values - average
    variance = lax.optimization_barrier(jnp.mean(centred * centred, axis=-1, keepdims=True))
    return (centred * lax.rsqrt(variance + EPSILON) * scale_gain.astype(jnp.float32)).astype(jnp.bfloat16)

def gelu_exact(values):
    return jax.nn.gelu(values, approximate=False)

def project(normed, weight):
    flattened = normed.reshape(-1, normed.shape[-1])
    output = jnp.dot(flattened, weight, preferred_element_type=jnp.float32)
    return output.reshape(normed.shape[:-1] + (weight.shape[1],))

def attend(normed, w_qkv, w_out):
    groups, tokens, channels = normed.shape
    head_size = channels // HEADS
    qkv_all = project(normed, w_qkv).astype(jnp.bfloat16)
    heads_split = qkv_all.reshape(groups, tokens, 3, HEADS, head_size).astype(jnp.float32)
    scores = jnp.einsum('gthd,gshd->ghts', heads_split[:, :, 0], heads_split[:, :, 1]) * head_size ** (-0.5)
    weights = jax.nn.softmax(scores, axis=-1).astype(jnp.bfloat16)
    mixed = jnp.einsum('ghts,gshd->gthd', weights.astype(jnp.float32), heads_split[:, :, 2])
    mixed = mixed.astype(jnp.bfloat16).reshape(groups, tokens, channels)
    return project(mixed, w_out)

def feed_forward(resid, scale_gain, w_in, w_out):
    normed = layer_norm(resid, scale_gain)
    inner_act = gelu_exact(project(normed, w_in)).astype(jnp.bfloat16)
    return (resid.astype(jnp.float32) + project(inner_act, w_out)).astype(jnp.bfloat16)

def reference(features, gain_conv, w_expand, w_depth, w_project, gain_block, qkv_block, out_block, gain_bffn, ffn_in_block, ffn_out_block, gain_grid, qkv_grid, out_grid, gain_gffn, ffn_in_grid, ffn_out_grid):
    padded_rows = jnp.pad(features, ((1, 1), (0, 0), (0, 0)))

    def band_step(band_index):
        first_row = band_index * BLOCK
        rows_in = lax.dynamic_slice_in_dim(padded_rows, first_row, BLOCK + 2, 0)
        expanded = gelu_exact(project(layer_norm(rows_in, gain_conv), w_expand)).astype(jnp.bfloat16)
        widened = jnp.pad(expanded, ((0, 0), (1, 1), (0, 0)))
        summed = jnp.zeros((BLOCK, W, HID), jnp.float32)
        for row_tap in range(3):
            for col_tap in range(3):
                summed = summed + widened[row_tap:row_tap + BLOCK, col_tap:col_tap + W].astype(jnp.float32) * w_depth[row_tap, col_tap].astype(jnp.float32)
        depthwise = gelu_exact(summed).astype(jnp.bfloat16)
        conv_out = (rows_in[1:BLOCK + 1].astype(jnp.float32) + project(depthwise, w_project)).astype(jnp.bfloat16)
        windows = conv_out.reshape(BLOCK, W // BLOCK, BLOCK, C).transpose(1, 0, 2, 3).reshape(W // BLOCK, BLOCK * BLOCK, C)
        update = attend(layer_norm(windows, gain_block), qkv_block, out_block)
        mixed_after = (windows.astype(jnp.float32) + update).astype(jnp.bfloat16)
        mixed_after = feed_forward(mixed_after, gain_bffn, ffn_in_block, ffn_out_block)
        return mixed_after.reshape(W // BLOCK, BLOCK, BLOCK, C).transpose(1, 0, 2, 3).reshape(BLOCK, W, C)
    band_out = lax.map(band_step, jnp.arange(H // BLOCK, dtype=jnp.int32))
    block_out = band_out.reshape(H, W, C)
    arranged = block_out.reshape(G, STRIDE_R, G, STRIDE_C, C).transpose(1, 3, 0, 2, 4)

    def offset_step(offset_slab):
        tokens = offset_slab.reshape(STRIDE_C, G * G, C)
        update = attend(layer_norm(tokens, gain_grid), qkv_grid, out_grid).astype(jnp.bfloat16)
        mixed_after = (tokens.astype(jnp.float32) + update.astype(jnp.float32)).astype(jnp.bfloat16)
        mixed_after = feed_forward(mixed_after, gain_gffn, ffn_in_grid, ffn_out_grid)
        return mixed_after.reshape(STRIDE_C, G, G, C)
    grid_out = lax.map(offset_step, arranged)
    return grid_out.transpose(2, 0, 3, 1, 4).reshape(H, W, C)
```

```python
import jax
import jax.numpy as jnp
from jax import lax
from jax.sharding import PartitionSpec as P

HEADS = 6
BLOCK = 8
G = 16


EPSILON = 1e-05


def extended(block, sides, width):
    for axis, dim in sides:
        count = lax.axis_size(axis)
        forward = [(i, i + 1) for i in range(count - 1)]
        backward = [(target, source) for source, target in forward]
        low = lax.ppermute(
            lax.slice_in_dim(block, block.shape[dim] - width, None, axis=dim), axis, forward
        )
        high = lax.ppermute(lax.slice_in_dim(block, 0, width, axis=dim), axis, backward)
        block = jnp.concatenate([low, block, high], axis=dim)
    return block


def layer_norm(values, scale_gain):
    values = values.astype(jnp.float32)
    average = jnp.mean(values, axis=-1, keepdims=True)
    centred = values - average
    variance = jnp.mean(centred * centred, axis=-1, keepdims=True)
    return (centred * lax.rsqrt(variance + EPSILON) * scale_gain).astype(jnp.bfloat16)


def gelu_exact(values):
    return jax.nn.gelu(values, approximate=False)


def project(normed, weight):
    flattened = normed.reshape(-1, normed.shape[-1])
    output = jnp.dot(flattened, weight, preferred_element_type=jnp.float32)
    return output.reshape(normed.shape[:-1] + (weight.shape[1],))


def attend(normed, w_qkv, w_out):
    groups, tokens, channels = normed.shape
    head_size = channels // HEADS
    qkv_all = project(normed, w_qkv).astype(jnp.bfloat16)
    heads_split = qkv_all.reshape(groups, tokens, 3, HEADS, head_size)
    scores = jnp.einsum(
        "gthd,gshd->ghts",
        heads_split[:, :, 0],
        heads_split[:, :, 1],
        preferred_element_type=jnp.float32,
    ) * head_size ** (-0.5)
    weights = jax.nn.softmax(scores, axis=-1).astype(jnp.bfloat16)
    mixed = jnp.einsum(
        "ghts,gshd->gthd", weights, heads_split[:, :, 2], preferred_element_type=jnp.float32
    )
    mixed = mixed.astype(jnp.bfloat16).reshape(groups, tokens, channels)
    return project(mixed, w_out)


def feed_forward(resid, scale_gain, w_in, w_out):
    normed = layer_norm(resid, scale_gain)
    inner_act = gelu_exact(project(normed, w_in)).astype(jnp.bfloat16)
    return (resid.astype(jnp.float32) + project(inner_act, w_out)).astype(jnp.bfloat16)


def shards(
    features,
    gain_conv,
    w_expand,
    w_depth,
    w_project,
    gain_block,
    qkv_block,
    out_block,
    gain_bffn,
    ffn_in_block,
    ffn_out_block,
    gain_grid,
    qkv_grid,
    out_grid,
    gain_gffn,
    ffn_in_grid,
    ffn_out_grid,
):
    rows_count = lax.axis_size("rows")
    cols_count = lax.axis_size("cols")
    tile_rows, tile_cols, channels = features.shape
    hidden_width = w_expand.shape[1]

    def expand(cells):
        return gelu_exact(project(layer_norm(cells, gain_conv), w_expand)).astype(jnp.bfloat16)

    border = extended(features, (("rows", 0), ("cols", 1)), 1)
    interior = expand(features)
    halo_cells = jnp.concatenate(
        [
            border[0, 1 : tile_cols + 1],
            border[tile_rows + 1, 1 : tile_cols + 1],
            border[:, 0],
            border[:, tile_cols + 1],
        ],
        axis=0,
    )
    halo = expand(halo_cells)
    top = halo[:tile_cols][None]
    bottom = halo[tile_cols : 2 * tile_cols][None]
    left = halo[2 * tile_cols : 2 * tile_cols + tile_rows + 2][:, None]
    right = halo[2 * tile_cols + tile_rows + 2 :][:, None]
    expanded = jnp.concatenate([top, interior, bottom], axis=0)
    expanded = jnp.concatenate([left, expanded, right], axis=1)
    summed = jnp.zeros((tile_rows, tile_cols, hidden_width), jnp.float32)
    for row_tap in range(3):
        for col_tap in range(3):
            summed = summed + expanded[
                row_tap : row_tap + tile_rows, col_tap : col_tap + tile_cols
            ].astype(jnp.float32) * w_depth[row_tap, col_tap].astype(jnp.float32)
    depthwise = gelu_exact(summed).astype(jnp.bfloat16)
    conv_out = (features.astype(jnp.float32) + project(depthwise, w_project)).astype(jnp.bfloat16)
    win_rows = tile_rows // BLOCK
    win_cols = tile_cols // BLOCK
    windows = (
        conv_out.reshape(win_rows, BLOCK, win_cols, BLOCK, channels)
        .transpose(0, 2, 1, 3, 4)
        .reshape(win_rows * win_cols, BLOCK * BLOCK, channels)
    )
    update = attend(layer_norm(windows, gain_block), qkv_block, out_block)
    mixed_after = (windows.astype(jnp.float32) + update).astype(jnp.bfloat16)
    mixed_after = feed_forward(mixed_after, gain_bffn, ffn_in_block, ffn_out_block)
    block_out = (
        mixed_after.reshape(win_rows, win_cols, BLOCK, BLOCK, channels)
        .transpose(0, 2, 1, 3, 4)
        .reshape(tile_rows, tile_cols, channels)
    )
    normed_grid = layer_norm(block_out, gain_grid)
    local_rows = G // rows_count
    local_cols = G // cols_count
    stride_rows = tile_rows // local_rows
    stride_cols = tile_cols // local_cols
    part_rows = stride_rows // rows_count
    part_cols = stride_cols // cols_count
    both = ("rows", "cols")
    devices = rows_count * cols_count
    split = normed_grid.reshape(
        local_rows, rows_count, part_rows, local_cols, cols_count, part_cols, channels
    ).transpose(1, 4, 2, 5, 0, 3, 6)
    split = split.reshape(devices, part_rows, part_cols, local_rows * local_cols, channels)
    received = lax.all_to_all(split, both, split_axis=0, concat_axis=3, tiled=True)
    answer = attend(
        received.reshape(part_rows * part_cols, G * G, channels), qkv_grid, out_grid
    ).astype(jnp.bfloat16)
    answer = answer.reshape(1, part_rows, part_cols, G * G, channels)
    returned = lax.all_to_all(answer, both, split_axis=3, concat_axis=0, tiled=True)
    restored = (
        returned.reshape(
            rows_count, cols_count, part_rows, part_cols, local_rows, local_cols, channels
        )
        .transpose(4, 0, 2, 5, 1, 3, 6)
        .reshape(tile_rows, tile_cols, channels)
    )
    grid_attn = (block_out.astype(jnp.float32) + restored.astype(jnp.float32)).astype(jnp.bfloat16)
    return feed_forward(grid_attn, gain_gffn, ffn_in_grid, ffn_out_grid)


def solution(mesh):
    return jax.shard_map(
        shards,
        mesh=mesh,
        in_specs=(
            P("rows", "cols", None),
            P(),
            P(),
            P(),
            P(),
            P(),
            P(),
            P(),
            P(),
            P(),
            P(),
            P(),
            P(),
            P(),
            P(),
            P(),
            P(),
        ),
        out_specs=P("rows", "cols", None),
        check_vma=False,
    )
```

```python
import jax
import jax.numpy as jnp
from jax import lax
from jax.sharding import PartitionSpec as P

HEADS = 6
BLOCK = 8
G = 16


EPSILON = 1e-05


def extended(block, sides, width):
    for axis, dim in sides:
        count = lax.axis_size(axis)
        forward = [(i, i + 1) for i in range(count - 1)]
        backward = [(target, source) for source, target in forward]
        low = lax.ppermute(
            lax.slice_in_dim(block, block.shape[dim] - width, None, axis=dim), axis, forward
        )
        high = lax.ppermute(lax.slice_in_dim(block, 0, width, axis=dim), axis, backward)
        block = jnp.concatenate([low, block, high], axis=dim)
    return block


def layer_norm(values, scale_gain):
    values = values.astype(jnp.float32)
    average = jnp.mean(values, axis=-1, keepdims=True)
    centred = values - average
    variance = jnp.mean(centred * centred, axis=-1, keepdims=True)
    return (centred * lax.rsqrt(variance + EPSILON) * scale_gain).astype(jnp.bfloat16)


def gelu_exact(values):
    return jax.nn.gelu(values, approximate=False)


def project(normed, weight):
    flattened = normed.reshape(-1, normed.shape[-1])
    output = jnp.dot(flattened, weight, preferred_element_type=jnp.float32)
    return output.reshape(normed.shape[:-1] + (weight.shape[1],))


def attend(normed, w_qkv, w_out):
    groups, tokens, channels = normed.shape
    head_size = channels // HEADS
    qkv_all = project(normed, w_qkv).astype(jnp.bfloat16)
    heads_split = qkv_all.reshape(groups, tokens, 3, HEADS, head_size)
    scores = jnp.einsum(
        "gthd,gshd->ghts",
        heads_split[:, :, 0],
        heads_split[:, :, 1],
        preferred_element_type=jnp.float32,
    ) * head_size ** (-0.5)
    weights = jax.nn.softmax(scores, axis=-1).astype(jnp.bfloat16)
    mixed = jnp.einsum(
        "ghts,gshd->gthd", weights, heads_split[:, :, 2], preferred_element_type=jnp.float32
    )
    mixed = mixed.astype(jnp.bfloat16).reshape(groups, tokens, channels)
    return project(mixed, w_out)


def feed_forward(resid, scale_gain, w_in, w_out):
    normed = layer_norm(resid, scale_gain)
    inner_act = gelu_exact(project(normed, w_in)).astype(jnp.bfloat16)
    return (resid.astype(jnp.float32) + project(inner_act, w_out)).astype(jnp.bfloat16)


def shards(
    features,
    gain_conv,
    w_expand,
    w_depth,
    w_project,
    gain_block,
    qkv_block,
    out_block,
    gain_bffn,
    ffn_in_block,
    ffn_out_block,
    gain_grid,
    qkv_grid,
    out_grid,
    gain_gffn,
    ffn_in_grid,
    ffn_out_grid,
):
    rows_count = lax.axis_size("rows")
    cols_count = lax.axis_size("cols")
    tile_rows, tile_cols, channels = features.shape
    hidden_width = w_expand.shape[1]

    def expand(cells):
        return gelu_exact(project(layer_norm(cells, gain_conv), w_expand)).astype(jnp.bfloat16)

    both = ("rows", "cols")
    row_index = lax.axis_index("rows")
    col_index = lax.axis_index("cols")

    def neighbour(piece, row_step, col_step):
        pairs = []
        for r in range(rows_count):
            for c in range(cols_count):
                source_r, source_c = r + row_step, c + col_step
                if 0 <= source_r < rows_count and 0 <= source_c < cols_count:
                    pairs.append((source_r * cols_count + source_c, r * cols_count + c))
        return lax.ppermute(piece, both, pairs)

    last_r, last_c = tile_rows - 1, tile_cols - 1
    halo_cells = jnp.concatenate(
        [
            neighbour(features[last_r], -1, 0),
            neighbour(features[0], 1, 0),
            neighbour(features[:, last_c], 0, -1),
            neighbour(features[:, 0], 0, 1),
            neighbour(features[last_r, last_c][None], -1, -1),
            neighbour(features[last_r, 0][None], -1, 1),
            neighbour(features[0, last_c][None], 1, -1),
            neighbour(features[0, 0][None], 1, 1),
        ],
        axis=0,
    )
    interior = expand(features)
    halo = expand(halo_cells)
    top = halo[:tile_cols]
    bottom = halo[tile_cols : 2 * tile_cols]
    left = halo[2 * tile_cols : 2 * tile_cols + tile_rows]
    right = halo[2 * tile_cols + tile_rows : 2 * tile_cols + 2 * tile_rows]
    corners = halo[2 * tile_cols + 2 * tile_rows :]
    top = jnp.concatenate([corners[0:1], top, corners[1:2]], axis=0)[None]
    bottom = jnp.concatenate([corners[2:3], bottom, corners[3:4]], axis=0)[None]
    middle = jnp.concatenate([left[:, None], interior, right[:, None]], axis=1)
    expanded = jnp.concatenate([top, middle, bottom], axis=0)
    summed = jnp.zeros((tile_rows, tile_cols, hidden_width), jnp.float32)
    for row_tap in range(3):
        for col_tap in range(3):
            summed = summed + expanded[
                row_tap : row_tap + tile_rows, col_tap : col_tap + tile_cols
            ].astype(jnp.float32) * w_depth[row_tap, col_tap].astype(jnp.float32)
    depthwise = gelu_exact(summed).astype(jnp.bfloat16)
    conv_out = (features.astype(jnp.float32) + project(depthwise, w_project)).astype(jnp.bfloat16)
    win_rows = tile_rows // BLOCK
    win_cols = tile_cols // BLOCK
    windows = (
        conv_out.reshape(win_rows, BLOCK, win_cols, BLOCK, channels)
        .transpose(0, 2, 1, 3, 4)
        .reshape(win_rows * win_cols, BLOCK * BLOCK, channels)
    )
    update = attend(layer_norm(windows, gain_block), qkv_block, out_block)
    mixed_after = (windows.astype(jnp.float32) + update).astype(jnp.bfloat16)
    mixed_after = feed_forward(mixed_after, gain_bffn, ffn_in_block, ffn_out_block)
    block_out = (
        mixed_after.reshape(win_rows, win_cols, BLOCK, BLOCK, channels)
        .transpose(0, 2, 1, 3, 4)
        .reshape(tile_rows, tile_cols, channels)
    )
    local_rows = G // rows_count
    local_cols = G // cols_count
    stride_rows = tile_rows // local_rows
    stride_cols = tile_cols // local_cols
    part_rows = stride_rows // rows_count
    part_cols = stride_cols // cols_count
    devices = rows_count * cols_count
    split = block_out.reshape(
        local_rows, rows_count, part_rows, local_cols, cols_count, part_cols, channels
    ).transpose(1, 4, 2, 5, 0, 3, 6)
    split = split.reshape(devices, part_rows, part_cols, local_rows * local_cols, channels)
    received = lax.all_to_all(split, both, split_axis=0, concat_axis=3, tiled=True)
    tokens = received.reshape(part_rows * part_cols, G * G, channels)
    update = attend(layer_norm(tokens, gain_grid), qkv_grid, out_grid).astype(jnp.bfloat16)
    grid_attn = (tokens.astype(jnp.float32) + update.astype(jnp.float32)).astype(jnp.bfloat16)
    grid_out = feed_forward(grid_attn, gain_gffn, ffn_in_grid, ffn_out_grid)
    grid_out = grid_out.reshape(1, part_rows, part_cols, G * G, channels)
    returned = lax.all_to_all(grid_out, both, split_axis=3, concat_axis=0, tiled=True)
    return (
        returned.reshape(
            rows_count, cols_count, part_rows, part_cols, local_rows, local_cols, channels
        )
        .transpose(4, 0, 2, 5, 1, 3, 6)
        .reshape(tile_rows, tile_cols, channels)
    )


def solution(mesh):
    return jax.shard_map(
        shards,
        mesh=mesh,
        in_specs=(
            P("rows", "cols", None),
            P(),
            P(),
            P(),
            P(),
            P(),
            P(),
            P(),
            P(),
            P(),
            P(),
            P(),
            P(),
            P(),
            P(),
            P(),
            P(),
        ),
        out_specs=P("rows", "cols", None),
        check_vma=False,
    )
```

```python
import jax
import jax.numpy as jnp
from jax import lax
from jax.sharding import PartitionSpec as P

HEADS = 6
BLOCK = 8
G = 16


EPSILON = 1e-05


def extended(block, sides, width):
    for axis, dim in sides:
        count = lax.axis_size(axis)
        forward = [(i, i + 1) for i in range(count - 1)]
        backward = [(target, source) for source, target in forward]
        low = lax.ppermute(
            lax.slice_in_dim(block, block.shape[dim] - width, None, axis=dim), axis, forward
        )
        high = lax.ppermute(lax.slice_in_dim(block, 0, width, axis=dim), axis, backward)
        block = jnp.concatenate([low, block, high], axis=dim)
    return block


def layer_norm(values, scale_gain):
    values = values.astype(jnp.float32)
    average = jnp.mean(values, axis=-1, keepdims=True)
    centred = values - average
    variance = jnp.mean(centred * centred, axis=-1, keepdims=True)
    return (centred * lax.rsqrt(variance + EPSILON) * scale_gain).astype(jnp.bfloat16)


def gelu_exact(values):
    return jax.nn.gelu(values, approximate=False)


def project(normed, weight):
    flattened = normed.reshape(-1, normed.shape[-1])
    output = jnp.dot(flattened, weight, preferred_element_type=jnp.float32)
    return output.reshape(normed.shape[:-1] + (weight.shape[1],))


def attend(normed, w_qkv, w_out):
    groups, tokens, channels = normed.shape
    head_size = channels // HEADS
    qkv_all = project(normed, w_qkv).astype(jnp.bfloat16)
    heads_split = qkv_all.reshape(groups, tokens, 3, HEADS, head_size)
    scores = jnp.einsum(
        "gthd,gshd->ghts",
        heads_split[:, :, 0],
        heads_split[:, :, 1],
        preferred_element_type=jnp.float32,
    ) * head_size ** (-0.5)
    weights = jax.nn.softmax(scores, axis=-1).astype(jnp.bfloat16)
    mixed = jnp.einsum(
        "ghts,gshd->gthd", weights, heads_split[:, :, 2], preferred_element_type=jnp.float32
    )
    mixed = mixed.astype(jnp.bfloat16).reshape(groups, tokens, channels)
    return project(mixed, w_out)


def feed_forward(resid, scale_gain, w_in, w_out):
    normed = layer_norm(resid, scale_gain)
    inner_act = gelu_exact(project(normed, w_in)).astype(jnp.bfloat16)
    return (resid.astype(jnp.float32) + project(inner_act, w_out)).astype(jnp.bfloat16)


def shards(
    features,
    gain_conv,
    w_expand,
    w_depth,
    w_project,
    gain_block,
    qkv_block,
    out_block,
    gain_bffn,
    ffn_in_block,
    ffn_out_block,
    gain_grid,
    qkv_grid,
    out_grid,
    gain_gffn,
    ffn_in_grid,
    ffn_out_grid,
):
    rows_count = lax.axis_size("rows")
    cols_count = lax.axis_size("cols")
    tile_rows, tile_cols, channels = features.shape
    hidden_width = w_expand.shape[1]

    def expand(cells):
        return gelu_exact(project(layer_norm(cells, gain_conv), w_expand)).astype(jnp.bfloat16)

    both = ("rows", "cols")
    border = extended(features, (("rows", 0), ("cols", 1)), 1)
    interior = expand(features)
    halo_cells = jnp.concatenate(
        [
            border[0, 1 : tile_cols + 1],
            border[tile_rows + 1, 1 : tile_cols + 1],
            border[:, 0],
            border[:, tile_cols + 1],
        ],
        axis=0,
    )
    halo = expand(halo_cells)
    top = halo[:tile_cols][None]
    bottom = halo[tile_cols : 2 * tile_cols][None]
    left = halo[2 * tile_cols : 2 * tile_cols + tile_rows + 2][:, None]
    right = halo[2 * tile_cols + tile_rows + 2 :][:, None]
    expanded = jnp.concatenate([top, interior, bottom], axis=0)
    expanded = jnp.concatenate([left, expanded, right], axis=1)
    summed = jnp.zeros((tile_rows, tile_cols, hidden_width), jnp.float32)
    for row_tap in range(3):
        for col_tap in range(3):
            summed = summed + expanded[
                row_tap : row_tap + tile_rows, col_tap : col_tap + tile_cols
            ].astype(jnp.float32) * w_depth[row_tap, col_tap].astype(jnp.float32)
    depthwise = gelu_exact(summed).astype(jnp.bfloat16)
    conv_out = (features.astype(jnp.float32) + project(depthwise, w_project)).astype(jnp.bfloat16)
    win_rows = tile_rows // BLOCK
    win_cols = tile_cols // BLOCK
    windows = (
        conv_out.reshape(win_rows, BLOCK, win_cols, BLOCK, channels)
        .transpose(0, 2, 1, 3, 4)
        .reshape(win_rows * win_cols, BLOCK * BLOCK, channels)
    )
    update = attend(layer_norm(windows, gain_block), qkv_block, out_block)
    mixed_after = (windows.astype(jnp.float32) + update).astype(jnp.bfloat16)
    mixed_after = feed_forward(mixed_after, gain_bffn, ffn_in_block, ffn_out_block)
    block_out = (
        mixed_after.reshape(win_rows, win_cols, BLOCK, BLOCK, channels)
        .transpose(0, 2, 1, 3, 4)
        .reshape(tile_rows, tile_cols, channels)
    )
    local_rows = G // rows_count
    local_cols = G // cols_count
    stride_rows = tile_rows // local_rows
    stride_cols = tile_cols // local_cols
    part_rows = stride_rows // rows_count
    part_cols = stride_cols // cols_count
    devices = rows_count * cols_count
    split = block_out.reshape(
        local_rows, rows_count, part_rows, local_cols, cols_count, part_cols, channels
    ).transpose(1, 4, 2, 5, 0, 3, 6)
    piece = (part_rows, part_cols, local_rows * local_cols, channels)
    packed = split.reshape(devices, -1, 128)
    received = lax.all_to_all(packed, both, split_axis=0, concat_axis=0, tiled=True)
    tokens = (
        received.reshape((devices,) + piece)
        .transpose(1, 2, 0, 3, 4)
        .reshape(part_rows * part_cols, G * G, channels)
    )
    update = attend(layer_norm(tokens, gain_grid), qkv_grid, out_grid).astype(jnp.bfloat16)
    grid_attn = (tokens.astype(jnp.float32) + update.astype(jnp.float32)).astype(jnp.bfloat16)
    grid_out = feed_forward(grid_attn, gain_gffn, ffn_in_grid, ffn_out_grid)
    grid_out = grid_out.reshape(part_rows, part_cols, devices, local_rows * local_cols, channels)
    packed = grid_out.transpose(2, 0, 1, 3, 4).reshape(devices, -1, 128)
    returned = lax.all_to_all(packed, both, split_axis=0, concat_axis=0, tiled=True)
    return (
        returned.reshape(
            rows_count, cols_count, part_rows, part_cols, local_rows, local_cols, channels
        )
        .transpose(4, 0, 2, 5, 1, 3, 6)
        .reshape(tile_rows, tile_cols, channels)
    )


def solution(mesh):
    return jax.shard_map(
        shards,
        mesh=mesh,
        in_specs=(
            P("rows", "cols", None),
            P(),
            P(),
            P(),
            P(),
            P(),
            P(),
            P(),
            P(),
            P(),
            P(),
            P(),
            P(),
            P(),
            P(),
            P(),
            P(),
        ),
        out_specs=P("rows", "cols", None),
        check_vma=False,
    )
```

```python
import jax
import jax.numpy as jnp
from jax import lax
from jax.sharding import PartitionSpec as P

HEADS = 6
BLOCK = 8
G = 16


EPSILON = 1e-05


def extended(block, sides, width):
    for axis, dim in sides:
        count = lax.axis_size(axis)
        forward = [(i, i + 1) for i in range(count - 1)]
        backward = [(target, source) for source, target in forward]
        low = lax.ppermute(
            lax.slice_in_dim(block, block.shape[dim] - width, None, axis=dim), axis, forward
        )
        high = lax.ppermute(lax.slice_in_dim(block, 0, width, axis=dim), axis, backward)
        block = jnp.concatenate([low, block, high], axis=dim)
    return block


def layer_norm(values, scale_gain):
    values = values.astype(jnp.float32)
    average = jnp.mean(values, axis=-1, keepdims=True)
    centred = values - average
    variance = jnp.mean(centred * centred, axis=-1, keepdims=True)
    return (centred * lax.rsqrt(variance + EPSILON) * scale_gain).astype(jnp.bfloat16)


def gelu_exact(values):
    return jax.nn.gelu(values, approximate=False)


def project(normed, weight):
    flattened = normed.reshape(-1, normed.shape[-1])
    output = jnp.dot(flattened, weight, preferred_element_type=jnp.float32)
    return output.reshape(normed.shape[:-1] + (weight.shape[1],))


def attend(normed, w_qkv, w_out):
    groups, tokens, channels = normed.shape
    head_size = channels // HEADS
    qkv_all = project(normed, w_qkv).astype(jnp.bfloat16)
    heads_split = qkv_all.reshape(groups, tokens, 3, HEADS, head_size)
    scores = jnp.einsum(
        "gthd,gshd->ghts",
        heads_split[:, :, 0],
        heads_split[:, :, 1],
        preferred_element_type=jnp.float32,
    ) * head_size ** (-0.5)
    weights = jax.nn.softmax(scores, axis=-1).astype(jnp.bfloat16)
    mixed = jnp.einsum(
        "ghts,gshd->gthd", weights, heads_split[:, :, 2], preferred_element_type=jnp.float32
    )
    mixed = mixed.astype(jnp.bfloat16).reshape(groups, tokens, channels)
    return project(mixed, w_out)


def feed_forward(resid, scale_gain, w_in, w_out):
    normed = layer_norm(resid, scale_gain)
    inner_act = gelu_exact(project(normed, w_in)).astype(jnp.bfloat16)
    return (resid.astype(jnp.float32) + project(inner_act, w_out)).astype(jnp.bfloat16)


def shards(
    features,
    gain_conv,
    w_expand,
    w_depth,
    w_project,
    gain_block,
    qkv_block,
    out_block,
    gain_bffn,
    ffn_in_block,
    ffn_out_block,
    gain_grid,
    qkv_grid,
    out_grid,
    gain_gffn,
    ffn_in_grid,
    ffn_out_grid,
):
    rows_count = lax.axis_size("rows")
    cols_count = lax.axis_size("cols")
    tile_rows, tile_cols, channels = features.shape
    hidden_width = w_expand.shape[1]

    def expand(cells):
        return gelu_exact(project(layer_norm(cells, gain_conv), w_expand)).astype(jnp.bfloat16)

    both = ("rows", "cols")
    border = extended(features, (("rows", 0), ("cols", 1)), 1)
    interior = expand(features)
    halo_cells = jnp.concatenate(
        [
            border[0, 1 : tile_cols + 1],
            border[tile_rows + 1, 1 : tile_cols + 1],
            border[:, 0],
            border[:, tile_cols + 1],
        ],
        axis=0,
    )
    halo = expand(halo_cells)
    top = halo[:tile_cols][None]
    bottom = halo[tile_cols : 2 * tile_cols][None]
    left = halo[2 * tile_cols : 2 * tile_cols + tile_rows + 2][:, None]
    right = halo[2 * tile_cols + tile_rows + 2 :][:, None]
    expanded = jnp.concatenate([top, interior, bottom], axis=0)
    expanded = jnp.concatenate([left, expanded, right], axis=1)
    summed = jnp.zeros((tile_rows, tile_cols, hidden_width), jnp.float32)
    for row_tap in range(3):
        for col_tap in range(3):
            summed = summed + expanded[
                row_tap : row_tap + tile_rows, col_tap : col_tap + tile_cols
            ].astype(jnp.float32) * w_depth[row_tap, col_tap].astype(jnp.float32)
    depthwise = gelu_exact(summed).astype(jnp.bfloat16)
    conv_out = (features.astype(jnp.float32) + project(depthwise, w_project)).astype(jnp.bfloat16)
    win_rows = tile_rows // BLOCK
    win_cols = tile_cols // BLOCK
    windows = (
        conv_out.reshape(win_rows, BLOCK, win_cols, BLOCK, channels)
        .transpose(0, 2, 1, 3, 4)
        .reshape(win_rows * win_cols, BLOCK * BLOCK, channels)
    )
    windows = lax.optimization_barrier(windows)
    update = attend(layer_norm(windows, gain_block), qkv_block, out_block)
    mixed_after = (windows.astype(jnp.float32) + update).astype(jnp.bfloat16)
    mixed_after = feed_forward(mixed_after, gain_bffn, ffn_in_block, ffn_out_block)
    block_out = (
        mixed_after.reshape(win_rows, win_cols, BLOCK, BLOCK, channels)
        .transpose(0, 2, 1, 3, 4)
        .reshape(tile_rows, tile_cols, channels)
    )
    local_rows = G // rows_count
    local_cols = G // cols_count
    stride_rows = tile_rows // local_rows
    stride_cols = tile_cols // local_cols
    part_rows = stride_rows // rows_count
    part_cols = stride_cols // cols_count
    devices = rows_count * cols_count
    split = block_out.reshape(
        local_rows, rows_count, part_rows, local_cols, cols_count, part_cols, channels
    ).transpose(1, 4, 2, 5, 0, 3, 6)
    piece = (part_rows, part_cols, local_rows * local_cols, channels)
    packed = split.reshape(devices, -1, 128)
    received = lax.all_to_all(packed, both, split_axis=0, concat_axis=0, tiled=True)
    tokens = (
        received.reshape((devices,) + piece)
        .transpose(1, 2, 0, 3, 4)
        .reshape(part_rows * part_cols, G * G, channels)
    )
    tokens = lax.optimization_barrier(tokens)
    update = attend(layer_norm(tokens, gain_grid), qkv_grid, out_grid).astype(jnp.bfloat16)
    grid_attn = (tokens.astype(jnp.float32) + update.astype(jnp.float32)).astype(jnp.bfloat16)
    grid_out = feed_forward(grid_attn, gain_gffn, ffn_in_grid, ffn_out_grid)
    grid_out = grid_out.reshape(part_rows, part_cols, devices, local_rows * local_cols, channels)
    packed = grid_out.transpose(2, 0, 1, 3, 4).reshape(devices, -1, 128)
    returned = lax.all_to_all(packed, both, split_axis=0, concat_axis=0, tiled=True)
    return (
        returned.reshape(
            rows_count, cols_count, part_rows, part_cols, local_rows, local_cols, channels
        )
        .transpose(4, 0, 2, 5, 1, 3, 6)
        .reshape(tile_rows, tile_cols, channels)
    )


def solution(mesh):
    return jax.shard_map(
        shards,
        mesh=mesh,
        in_specs=(
            P("rows", "cols", None),
            P(),
            P(),
            P(),
            P(),
            P(),
            P(),
            P(),
            P(),
            P(),
            P(),
            P(),
            P(),
            P(),
            P(),
            P(),
            P(),
        ),
        out_specs=P("rows", "cols", None),
        check_vma=False,
    )
```

```python
import jax
import jax.numpy as jnp
import numpy as np
from jax import lax
from jax.sharding import PartitionSpec as P

HEADS = 6
BLOCK = 8
G = 16


EPSILON = 1e-05


def layer_norm(values, scale_gain):
    values = values.astype(jnp.float32)
    average = jnp.mean(values, axis=-1, keepdims=True)
    centred = values - average
    variance = jnp.mean(centred * centred, axis=-1, keepdims=True)
    return (centred * lax.rsqrt(variance + EPSILON) * scale_gain).astype(jnp.bfloat16)


def gelu_exact(values):
    sqrt_half = np.sqrt(0.5).astype(values.dtype)
    return 0.5 * values * (1.0 + lax.erf(values * sqrt_half))


def project(normed, weight):
    flattened = normed.reshape(-1, normed.shape[-1])
    output = jnp.dot(flattened, weight, preferred_element_type=jnp.float32)
    return output.reshape(normed.shape[:-1] + (weight.shape[1],))


def attend(normed, w_qkv, w_out):
    groups, tokens, channels = normed.shape
    head_size = channels // HEADS
    qkv_all = project(normed, w_qkv).astype(jnp.bfloat16)
    heads_split = qkv_all.reshape(groups, tokens, 3, HEADS, head_size)
    scores = jnp.einsum(
        "gthd,gshd->ghts",
        heads_split[:, :, 0],
        heads_split[:, :, 1],
        preferred_element_type=jnp.float32,
    ) * head_size ** (-0.5)
    weights = jax.nn.softmax(scores, axis=-1).astype(jnp.bfloat16)
    mixed = jnp.einsum(
        "ghts,gshd->gthd", weights, heads_split[:, :, 2], preferred_element_type=jnp.float32
    )
    mixed = mixed.astype(jnp.bfloat16).reshape(groups, tokens, channels)
    return project(mixed, w_out)


def feed_forward(resid, scale_gain, w_in, w_out):
    normed = layer_norm(resid, scale_gain)
    inner_act = gelu_exact(project(normed, w_in)).astype(jnp.bfloat16)
    return (resid.astype(jnp.float32) + project(inner_act, w_out)).astype(jnp.bfloat16)


def shards_body(
    features,
    gain_conv,
    w_expand,
    w_depth,
    w_project,
    gain_block,
    qkv_block,
    out_block,
    gain_bffn,
    ffn_in_block,
    ffn_out_block,
    gain_grid,
    qkv_grid,
    out_grid,
    gain_gffn,
    ffn_in_grid,
    ffn_out_grid,
):
    rows_count = lax.axis_size("rows")
    cols_count = lax.axis_size("cols")
    tile_rows, tile_cols, channels = features.shape
    hidden_width = w_expand.shape[1]

    def expand(cells):
        return gelu_exact(project(layer_norm(cells, gain_conv), w_expand)).astype(jnp.bfloat16)

    both = ("rows", "cols")
    row_forward = [(i, i + 1) for i in range(rows_count - 1)]
    row_backward = [(t, s) for s, t in row_forward]
    col_forward = [(i, i + 1) for i in range(cols_count - 1)]
    col_backward = [(t, s) for s, t in col_forward]
    last_r, last_c = tile_rows - 1, tile_cols - 1
    top_row = lax.ppermute(features[last_r], "rows", row_forward)
    bottom_row = lax.ppermute(features[0], "rows", row_backward)
    left_source = jnp.concatenate(
        [top_row[last_c:], features[:, last_c], bottom_row[last_c:]], axis=0
    )
    right_source = jnp.concatenate([top_row[:1], features[:, 0], bottom_row[:1]], axis=0)
    left_col = lax.ppermute(left_source, "cols", col_forward)
    right_col = lax.ppermute(right_source, "cols", col_backward)
    interior_normed = layer_norm(features, gain_conv)
    interior = gelu_exact(project(interior_normed, w_expand)).astype(jnp.bfloat16)
    halo_cells = jnp.concatenate([top_row, bottom_row, left_col, right_col], axis=0)
    halo = expand(halo_cells)
    top = halo[:tile_cols][None]
    bottom = halo[tile_cols : 2 * tile_cols][None]
    left = halo[2 * tile_cols : 2 * tile_cols + tile_rows + 2][:, None]
    right = halo[2 * tile_cols + tile_rows + 2 :][:, None]
    expanded = jnp.concatenate([top, interior, bottom], axis=0)
    expanded = jnp.concatenate([left, expanded, right], axis=1)
    summed = jnp.zeros((tile_rows, tile_cols, hidden_width), jnp.float32)
    for row_tap in range(3):
        for col_tap in range(3):
            summed = summed + expanded[
                row_tap : row_tap + tile_rows, col_tap : col_tap + tile_cols
            ].astype(jnp.float32) * w_depth[row_tap, col_tap].astype(jnp.float32)
    depthwise = gelu_exact(summed).astype(jnp.bfloat16)
    conv_out = (features.astype(jnp.float32) + project(depthwise, w_project)).astype(jnp.bfloat16)
    win_rows = tile_rows // BLOCK
    win_cols = tile_cols // BLOCK
    windows = (
        conv_out.reshape(win_rows, BLOCK, win_cols, BLOCK, channels)
        .transpose(0, 2, 1, 3, 4)
        .reshape(win_rows * win_cols, BLOCK * BLOCK, channels)
    )
    windows = lax.optimization_barrier(windows)
    update = attend(layer_norm(windows, gain_block), qkv_block, out_block)
    mixed_after = (windows.astype(jnp.float32) + update).astype(jnp.bfloat16)
    mixed_after = feed_forward(mixed_after, gain_bffn, ffn_in_block, ffn_out_block)
    block_out = (
        mixed_after.reshape(win_rows, win_cols, BLOCK, BLOCK, channels)
        .transpose(0, 2, 1, 3, 4)
        .reshape(tile_rows, tile_cols, channels)
    )
    local_rows = G // rows_count
    local_cols = G // cols_count
    stride_rows = tile_rows // local_rows
    stride_cols = tile_cols // local_cols
    part_rows = stride_rows // rows_count
    part_cols = stride_cols // cols_count
    devices = rows_count * cols_count
    split = block_out.reshape(
        local_rows, rows_count, part_rows, local_cols, cols_count, part_cols, channels
    ).transpose(1, 4, 2, 5, 0, 3, 6)
    piece = (part_rows, part_cols, local_rows * local_cols, channels)
    packed = split.reshape(devices, -1, 128)
    received = lax.all_to_all(packed, both, split_axis=0, concat_axis=0, tiled=True)
    tokens = (
        received.reshape((devices,) + piece)
        .transpose(1, 2, 0, 3, 4)
        .reshape(part_rows * part_cols, G * G, channels)
    )
    tokens = lax.optimization_barrier(tokens)
    update = attend(layer_norm(tokens, gain_grid), qkv_grid, out_grid).astype(jnp.bfloat16)
    grid_attn = (tokens.astype(jnp.float32) + update.astype(jnp.float32)).astype(jnp.bfloat16)
    grid_out = feed_forward(grid_attn, gain_gffn, ffn_in_grid, ffn_out_grid)
    grid_out = grid_out.reshape(part_rows, part_cols, devices, local_rows * local_cols, channels)
    packed = grid_out.transpose(2, 0, 1, 3, 4).reshape(devices, -1, 128)
    returned = lax.all_to_all(packed, both, split_axis=0, concat_axis=0, tiled=True)
    return (
        returned.reshape(
            rows_count, cols_count, part_rows, part_cols, local_rows, local_cols, channels
        )
        .transpose(4, 0, 2, 5, 1, 3, 6)
        .reshape(tile_rows, tile_cols, channels)
    )


def solution(mesh):
    return jax.shard_map(
        shards_body,
        mesh=mesh,
        in_specs=(
            P("rows", "cols", None),
            P(),
            P(),
            P(),
            P(),
            P(),
            P(),
            P(),
            P(),
            P(),
            P(),
            P(),
            P(),
            P(),
            P(),
            P(),
            P(),
        ),
        out_specs=P("rows", "cols", None),
        check_vma=False,
    )
```

```python
import jax
import jax.numpy as jnp
import numpy as np
from jax import lax
from jax.sharding import PartitionSpec as P

HEADS = 6
BLOCK = 8
G = 16


EPSILON = 1e-05


def layer_norm(values, scale_gain):
    values = values.astype(jnp.float32)
    average = jnp.mean(values, axis=-1, keepdims=True)
    centred = values - average
    variance = jnp.mean(centred * centred, axis=-1, keepdims=True)
    return (centred * lax.rsqrt(variance + EPSILON) * scale_gain).astype(jnp.bfloat16)


def gelu_exact(values):
    sqrt_half = np.sqrt(0.5).astype(values.dtype)
    return 0.5 * values * (1.0 + lax.erf(values * sqrt_half))


def project(normed, weight):
    flattened = normed.reshape(-1, normed.shape[-1])
    output = jnp.dot(flattened, weight, preferred_element_type=jnp.float32)
    return output.reshape(normed.shape[:-1] + (weight.shape[1],))


def attend(normed, w_qkv, w_out):
    groups, tokens, channels = normed.shape
    head_size = channels // HEADS
    qkv_all = project(normed, w_qkv).astype(jnp.bfloat16)
    heads_split = qkv_all.reshape(groups, tokens, 3, HEADS, head_size)
    scores = jnp.einsum(
        "gthd,gshd->ghts",
        heads_split[:, :, 0],
        heads_split[:, :, 1],
        preferred_element_type=jnp.float32,
    ) * head_size ** (-0.5)
    peak = jnp.max(scores, axis=-1, keepdims=True)
    lifted = jnp.exp(scores - peak)
    total = jnp.sum(lifted, axis=-1, keepdims=True)
    weights = (lifted * (1.0 / total)).astype(jnp.bfloat16)
    mixed = jnp.einsum(
        "ghts,gshd->gthd", weights, heads_split[:, :, 2], preferred_element_type=jnp.float32
    )
    mixed = mixed.astype(jnp.bfloat16).reshape(groups, tokens, channels)
    return project(mixed, w_out)


def feed_forward(resid, scale_gain, w_in, w_out):
    normed = layer_norm(resid, scale_gain)
    inner_act = gelu_exact(project(normed, w_in)).astype(jnp.bfloat16)
    return (resid.astype(jnp.float32) + project(inner_act, w_out)).astype(jnp.bfloat16)


def shards_body(
    features,
    gain_conv,
    w_expand,
    w_depth,
    w_project,
    gain_block,
    qkv_block,
    out_block,
    gain_bffn,
    ffn_in_block,
    ffn_out_block,
    gain_grid,
    qkv_grid,
    out_grid,
    gain_gffn,
    ffn_in_grid,
    ffn_out_grid,
):
    rows_count = lax.axis_size("rows")
    cols_count = lax.axis_size("cols")
    tile_rows, tile_cols, channels = features.shape
    hidden_width = w_expand.shape[1]

    def expand(cells):
        return gelu_exact(project(layer_norm(cells, gain_conv), w_expand)).astype(jnp.bfloat16)

    both = ("rows", "cols")
    row_forward = [(i, i + 1) for i in range(rows_count - 1)]
    row_backward = [(t, s) for s, t in row_forward]
    col_forward = [(i, i + 1) for i in range(cols_count - 1)]
    col_backward = [(t, s) for s, t in col_forward]
    last_r, last_c = tile_rows - 1, tile_cols - 1
    top_row = lax.ppermute(features[last_r], "rows", row_forward)
    bottom_row = lax.ppermute(features[0], "rows", row_backward)
    left_source = jnp.concatenate(
        [top_row[last_c:], features[:, last_c], bottom_row[last_c:]], axis=0
    )
    right_source = jnp.concatenate([top_row[:1], features[:, 0], bottom_row[:1]], axis=0)
    left_col = lax.ppermute(left_source, "cols", col_forward)
    right_col = lax.ppermute(right_source, "cols", col_backward)
    interior_normed = layer_norm(features, gain_conv)
    interior = gelu_exact(project(interior_normed, w_expand)).astype(jnp.bfloat16)
    halo_cells = jnp.concatenate([top_row, bottom_row, left_col, right_col], axis=0)
    halo = expand(halo_cells)
    top = halo[:tile_cols][None]
    bottom = halo[tile_cols : 2 * tile_cols][None]
    left = halo[2 * tile_cols : 2 * tile_cols + tile_rows + 2][:, None]
    right = halo[2 * tile_cols + tile_rows + 2 :][:, None]
    expanded = jnp.concatenate([top, interior, bottom], axis=0)
    expanded = jnp.concatenate([left, expanded, right], axis=1)
    summed = jnp.zeros((tile_rows, tile_cols, hidden_width), jnp.float32)
    for row_tap in range(3):
        for col_tap in range(3):
            summed = summed + expanded[
                row_tap : row_tap + tile_rows, col_tap : col_tap + tile_cols
            ].astype(jnp.float32) * w_depth[row_tap, col_tap].astype(jnp.float32)
    depthwise = gelu_exact(summed).astype(jnp.bfloat16)
    conv_out = (features.astype(jnp.float32) + project(depthwise, w_project)).astype(jnp.bfloat16)
    win_rows = tile_rows // BLOCK
    win_cols = tile_cols // BLOCK
    windows = (
        conv_out.reshape(win_rows, BLOCK, win_cols, BLOCK, channels)
        .transpose(0, 2, 1, 3, 4)
        .reshape(win_rows * win_cols, BLOCK * BLOCK, channels)
    )
    windows = lax.optimization_barrier(windows)
    update = attend(layer_norm(windows, gain_block), qkv_block, out_block)
    mixed_after = (windows.astype(jnp.float32) + update).astype(jnp.bfloat16)
    mixed_after = feed_forward(mixed_after, gain_bffn, ffn_in_block, ffn_out_block)
    block_out = (
        mixed_after.reshape(win_rows, win_cols, BLOCK, BLOCK, channels)
        .transpose(0, 2, 1, 3, 4)
        .reshape(tile_rows, tile_cols, channels)
    )
    local_rows = G // rows_count
    local_cols = G // cols_count
    stride_rows = tile_rows // local_rows
    stride_cols = tile_cols // local_cols
    part_rows = stride_rows // rows_count
    part_cols = stride_cols // cols_count
    devices = rows_count * cols_count
    split = block_out.reshape(
        local_rows, rows_count, part_rows, local_cols, cols_count, part_cols, channels
    ).transpose(1, 4, 2, 5, 0, 3, 6)
    piece = (part_rows, part_cols, local_rows * local_cols, channels)
    packed = split.reshape(devices, -1, 128)
    received = lax.all_to_all(packed, both, split_axis=0, concat_axis=0, tiled=True)
    tokens = (
        received.reshape((devices,) + piece)
        .transpose(1, 2, 0, 3, 4)
        .reshape(part_rows * part_cols, G * G, channels)
    )
    tokens = lax.optimization_barrier(tokens)
    update = attend(layer_norm(tokens, gain_grid), qkv_grid, out_grid).astype(jnp.bfloat16)
    grid_attn = (tokens.astype(jnp.float32) + update.astype(jnp.float32)).astype(jnp.bfloat16)
    grid_out = feed_forward(grid_attn, gain_gffn, ffn_in_grid, ffn_out_grid)
    grid_out = grid_out.reshape(part_rows, part_cols, devices, local_rows * local_cols, channels)
    packed = grid_out.transpose(2, 0, 1, 3, 4).reshape(devices, -1, 128)
    returned = lax.all_to_all(packed, both, split_axis=0, concat_axis=0, tiled=True)
    return (
        returned.reshape(
            rows_count, cols_count, part_rows, part_cols, local_rows, local_cols, channels
        )
        .transpose(4, 0, 2, 5, 1, 3, 6)
        .reshape(tile_rows, tile_cols, channels)
    )


def solution(mesh):
    return jax.shard_map(
        shards_body,
        mesh=mesh,
        in_specs=(
            P("rows", "cols", None),
            P(),
            P(),
            P(),
            P(),
            P(),
            P(),
            P(),
            P(),
            P(),
            P(),
            P(),
            P(),
            P(),
            P(),
            P(),
            P(),
        ),
        out_specs=P("rows", "cols", None),
        check_vma=False,
    )
```

```python
import jax
import jax.numpy as jnp
import numpy as np
from jax import lax
from jax.sharding import PartitionSpec as P

HEADS = 6
BLOCK = 8
G = 16


EPSILON = 1e-05


def layer_norm(values, scale_gain):
    values = values.astype(jnp.float32)
    average = jnp.mean(values, axis=-1, keepdims=True)
    centred = values - average
    variance = jnp.mean(centred * centred, axis=-1, keepdims=True)
    return (centred * lax.rsqrt(variance + EPSILON) * scale_gain).astype(jnp.bfloat16)


def gelu_exact(values):
    sqrt_half = np.sqrt(0.5).astype(values.dtype)
    return 0.5 * values * (1.0 + lax.erf(values * sqrt_half))


def project(normed, weight):
    flattened = normed.reshape(-1, normed.shape[-1])
    output = jnp.dot(flattened, weight, preferred_element_type=jnp.float32)
    return output.reshape(normed.shape[:-1] + (weight.shape[1],))


def attend(normed, w_qkv, w_out):
    groups, tokens, channels = normed.shape
    head_size = channels // HEADS
    w_split = w_qkv.reshape(channels, 3, HEADS, head_size)

    def heads_of(part):
        return jnp.einsum(
            "gtc,chd->ghtd", normed, w_split[:, part], preferred_element_type=jnp.float32
        ).astype(jnp.bfloat16)

    queries, keys, values = heads_of(0), heads_of(1), heads_of(2)
    scores = jnp.einsum(
        "ghtd,ghsd->ghts", queries, keys, preferred_element_type=jnp.float32
    ) * head_size ** (-0.5)
    peak = jnp.max(scores, axis=-1, keepdims=True)
    lifted = jnp.exp(scores - peak)
    total = jnp.sum(lifted, axis=-1, keepdims=True)
    weights = (lifted * (1.0 / total)).astype(jnp.bfloat16)
    mixed = jnp.einsum("ghts,ghsd->gthd", weights, values, preferred_element_type=jnp.float32)
    mixed = mixed.astype(jnp.bfloat16).reshape(groups, tokens, channels)
    return project(mixed, w_out)


def feed_forward(resid, scale_gain, w_in, w_out):
    normed = layer_norm(resid, scale_gain)
    inner_act = gelu_exact(project(normed, w_in)).astype(jnp.bfloat16)
    return (resid.astype(jnp.float32) + project(inner_act, w_out)).astype(jnp.bfloat16)


def shards_body(
    features,
    gain_conv,
    w_expand,
    w_depth,
    w_project,
    gain_block,
    qkv_block,
    out_block,
    gain_bffn,
    ffn_in_block,
    ffn_out_block,
    gain_grid,
    qkv_grid,
    out_grid,
    gain_gffn,
    ffn_in_grid,
    ffn_out_grid,
):
    rows_count = lax.axis_size("rows")
    cols_count = lax.axis_size("cols")
    tile_rows, tile_cols, channels = features.shape
    hidden_width = w_expand.shape[1]

    def expand(cells):
        return gelu_exact(project(layer_norm(cells, gain_conv), w_expand)).astype(jnp.bfloat16)

    both = ("rows", "cols")
    row_forward = [(i, i + 1) for i in range(rows_count - 1)]
    row_backward = [(t, s) for s, t in row_forward]
    col_forward = [(i, i + 1) for i in range(cols_count - 1)]
    col_backward = [(t, s) for s, t in col_forward]
    last_r, last_c = tile_rows - 1, tile_cols - 1
    top_row = lax.ppermute(features[last_r], "rows", row_forward)
    bottom_row = lax.ppermute(features[0], "rows", row_backward)
    left_source = jnp.concatenate(
        [top_row[last_c:], features[:, last_c], bottom_row[last_c:]], axis=0
    )
    right_source = jnp.concatenate([top_row[:1], features[:, 0], bottom_row[:1]], axis=0)
    left_col = lax.ppermute(left_source, "cols", col_forward)
    right_col = lax.ppermute(right_source, "cols", col_backward)
    interior_normed = layer_norm(features, gain_conv)
    interior = gelu_exact(project(interior_normed, w_expand)).astype(jnp.bfloat16)
    halo_cells = jnp.concatenate([top_row, bottom_row, left_col, right_col], axis=0)
    halo = expand(halo_cells)
    top = halo[:tile_cols][None]
    bottom = halo[tile_cols : 2 * tile_cols][None]
    left = halo[2 * tile_cols : 2 * tile_cols + tile_rows + 2][:, None]
    right = halo[2 * tile_cols + tile_rows + 2 :][:, None]
    expanded = jnp.concatenate([top, interior, bottom], axis=0)
    expanded = jnp.concatenate([left, expanded, right], axis=1)
    summed = jnp.zeros((tile_rows, tile_cols, hidden_width), jnp.float32)
    for row_tap in range(3):
        for col_tap in range(3):
            summed = summed + expanded[
                row_tap : row_tap + tile_rows, col_tap : col_tap + tile_cols
            ].astype(jnp.float32) * w_depth[row_tap, col_tap].astype(jnp.float32)
    depthwise = gelu_exact(summed).astype(jnp.bfloat16)
    conv_out = (features.astype(jnp.float32) + project(depthwise, w_project)).astype(jnp.bfloat16)
    win_rows = tile_rows // BLOCK
    win_cols = tile_cols // BLOCK
    windows = (
        conv_out.reshape(win_rows, BLOCK, win_cols, BLOCK, channels)
        .transpose(0, 2, 1, 3, 4)
        .reshape(win_rows * win_cols, BLOCK * BLOCK, channels)
    )
    windows = lax.optimization_barrier(windows)
    update = attend(layer_norm(windows, gain_block), qkv_block, out_block)
    mixed_after = (windows.astype(jnp.float32) + update).astype(jnp.bfloat16)
    mixed_after = feed_forward(mixed_after, gain_bffn, ffn_in_block, ffn_out_block)
    local_rows = G // rows_count
    local_cols = G // cols_count
    stride_rows = tile_rows // local_rows
    stride_cols = tile_cols // local_cols
    part_rows = stride_rows // rows_count
    part_cols = stride_cols // cols_count
    devices = rows_count * cols_count
    assert part_cols == BLOCK and BLOCK % part_rows == 0
    split = mixed_after.reshape(
        local_rows,
        win_rows // local_rows,
        local_cols,
        cols_count,
        BLOCK // part_rows,
        part_rows,
        BLOCK,
        channels,
    ).transpose(1, 4, 3, 5, 6, 0, 2, 7)
    piece = (part_rows, part_cols, local_rows * local_cols, channels)
    packed = split.reshape(devices, -1, 128)
    received = lax.all_to_all(packed, both, split_axis=0, concat_axis=0, tiled=True)
    tokens = (
        received.reshape((devices,) + piece)
        .transpose(1, 2, 0, 3, 4)
        .reshape(part_rows * part_cols, G * G, channels)
    )
    tokens = lax.optimization_barrier(tokens)
    update = attend(layer_norm(tokens, gain_grid), qkv_grid, out_grid).astype(jnp.bfloat16)
    grid_attn = (tokens.astype(jnp.float32) + update.astype(jnp.float32)).astype(jnp.bfloat16)
    grid_out = feed_forward(grid_attn, gain_gffn, ffn_in_grid, ffn_out_grid)
    grid_out = grid_out.reshape(part_rows, part_cols, devices, local_rows * local_cols, channels)
    packed = grid_out.transpose(2, 0, 1, 3, 4).reshape(devices, -1, 128)
    returned = lax.all_to_all(packed, both, split_axis=0, concat_axis=0, tiled=True)
    return (
        returned.reshape(
            rows_count, cols_count, part_rows, part_cols, local_rows, local_cols, channels
        )
        .transpose(4, 0, 2, 5, 1, 3, 6)
        .reshape(tile_rows, tile_cols, channels)
    )


def solution(mesh):
    return jax.shard_map(
        shards_body,
        mesh=mesh,
        in_specs=(
            P("rows", "cols", None),
            P(),
            P(),
            P(),
            P(),
            P(),
            P(),
            P(),
            P(),
            P(),
            P(),
            P(),
            P(),
            P(),
            P(),
            P(),
            P(),
        ),
        out_specs=P("rows", "cols", None),
        check_vma=False,
    )
```

```python
import jax
import jax.numpy as jnp
import numpy as np
from jax import lax
from jax.sharding import PartitionSpec as P

HEADS = 6
BLOCK = 8
G = 16


EPSILON = 1e-05


def layer_norm(values, scale_gain):
    values = values.astype(jnp.float32)
    average = jnp.mean(values, axis=-1, keepdims=True)
    centred = values - average
    variance = jnp.mean(centred * centred, axis=-1, keepdims=True)
    return (centred * lax.rsqrt(variance + EPSILON) * scale_gain).astype(jnp.bfloat16)


def gelu_exact(values):
    sqrt_half = np.sqrt(0.5).astype(values.dtype)
    return 0.5 * values * (1.0 + lax.erf(values * sqrt_half))


def project(normed, weight):
    flattened = normed.reshape(-1, normed.shape[-1])
    output = jnp.dot(flattened, weight, preferred_element_type=jnp.float32)
    return output.reshape(normed.shape[:-1] + (weight.shape[1],))


def attend(normed, w_qkv, w_out):
    groups, tokens, channels = normed.shape
    head_size = channels // HEADS
    w_split = w_qkv.reshape(channels, 3, HEADS, head_size)

    def heads_of(part):
        return jnp.einsum(
            "gtc,chd->ghtd", normed, w_split[:, part], preferred_element_type=jnp.float32
        ).astype(jnp.bfloat16)

    queries, keys, values = heads_of(0), heads_of(1), heads_of(2)

    def core(chunk):
        q, k, v = chunk
        scores = jnp.einsum(
            "ghtd,ghsd->ghts", q, k, preferred_element_type=jnp.float32
        ) * head_size ** (-0.5)
        peak = jnp.max(scores, axis=-1, keepdims=True)
        lifted = jnp.exp(scores - peak)
        total = jnp.sum(lifted, axis=-1, keepdims=True)
        weights = (lifted * (1.0 / total)).astype(jnp.bfloat16)
        mixed = jnp.einsum("ghts,ghsd->gthd", weights, v, preferred_element_type=jnp.float32)
        return mixed.astype(jnp.bfloat16)

    chunks = max(1, groups * tokens * tokens // (32 * 64 * 64))
    split = lambda a: a.reshape((chunks, groups // chunks) + a.shape[1:])
    mixed = lax.map(core, (split(queries), split(keys), split(values)))
    mixed = mixed.reshape(groups, tokens, channels)
    return project(mixed, w_out)


def feed_forward(resid, scale_gain, w_in, w_out):
    normed = layer_norm(resid, scale_gain)
    inner_act = gelu_exact(project(normed, w_in)).astype(jnp.bfloat16)
    return (resid.astype(jnp.float32) + project(inner_act, w_out)).astype(jnp.bfloat16)


def shards_body(
    features,
    gain_conv,
    w_expand,
    w_depth,
    w_project,
    gain_block,
    qkv_block,
    out_block,
    gain_bffn,
    ffn_in_block,
    ffn_out_block,
    gain_grid,
    qkv_grid,
    out_grid,
    gain_gffn,
    ffn_in_grid,
    ffn_out_grid,
):
    rows_count = lax.axis_size("rows")
    cols_count = lax.axis_size("cols")
    tile_rows, tile_cols, channels = features.shape
    hidden_width = w_expand.shape[1]

    def expand(cells):
        return gelu_exact(project(layer_norm(cells, gain_conv), w_expand)).astype(jnp.bfloat16)

    both = ("rows", "cols")
    row_forward = [(i, i + 1) for i in range(rows_count - 1)]
    row_backward = [(t, s) for s, t in row_forward]
    col_forward = [(i, i + 1) for i in range(cols_count - 1)]
    col_backward = [(t, s) for s, t in col_forward]
    last_r, last_c = tile_rows - 1, tile_cols - 1
    top_row = lax.ppermute(features[last_r], "rows", row_forward)
    bottom_row = lax.ppermute(features[0], "rows", row_backward)
    left_source = jnp.concatenate(
        [top_row[last_c:], features[:, last_c], bottom_row[last_c:]], axis=0
    )
    right_source = jnp.concatenate([top_row[:1], features[:, 0], bottom_row[:1]], axis=0)
    left_col = lax.ppermute(left_source, "cols", col_forward)
    right_col = lax.ppermute(right_source, "cols", col_backward)
    interior_normed = layer_norm(features, gain_conv)
    interior = gelu_exact(project(interior_normed, w_expand)).astype(jnp.bfloat16)
    halo_cells = jnp.concatenate([top_row, bottom_row, left_col, right_col], axis=0)
    halo = expand(halo_cells)
    top = halo[:tile_cols][None]
    bottom = halo[tile_cols : 2 * tile_cols][None]
    left = halo[2 * tile_cols : 2 * tile_cols + tile_rows + 2][:, None]
    right = halo[2 * tile_cols + tile_rows + 2 :][:, None]
    expanded = jnp.concatenate([top, interior, bottom], axis=0)
    expanded = jnp.concatenate([left, expanded, right], axis=1)
    summed = jnp.zeros((tile_rows, tile_cols, hidden_width), jnp.float32)
    for row_tap in range(3):
        for col_tap in range(3):
            summed = summed + expanded[
                row_tap : row_tap + tile_rows, col_tap : col_tap + tile_cols
            ].astype(jnp.float32) * w_depth[row_tap, col_tap].astype(jnp.float32)
    depthwise = gelu_exact(summed).astype(jnp.bfloat16)
    conv_out = (features.astype(jnp.float32) + project(depthwise, w_project)).astype(jnp.bfloat16)
    win_rows = tile_rows // BLOCK
    win_cols = tile_cols // BLOCK
    windows = (
        conv_out.reshape(win_rows, BLOCK, win_cols, BLOCK, channels)
        .transpose(0, 2, 1, 3, 4)
        .reshape(win_rows * win_cols, BLOCK * BLOCK, channels)
    )
    windows = lax.optimization_barrier(windows)
    update = attend(layer_norm(windows, gain_block), qkv_block, out_block)
    mixed_after = (windows.astype(jnp.float32) + update).astype(jnp.bfloat16)
    mixed_after = feed_forward(mixed_after, gain_bffn, ffn_in_block, ffn_out_block)
    block_out = (
        mixed_after.reshape(win_rows, win_cols, BLOCK, BLOCK, channels)
        .transpose(0, 2, 1, 3, 4)
        .reshape(tile_rows, tile_cols, channels)
    )
    local_rows = G // rows_count
    local_cols = G // cols_count
    stride_rows = tile_rows // local_rows
    stride_cols = tile_cols // local_cols
    part_rows = stride_rows // rows_count
    part_cols = stride_cols // cols_count
    devices = rows_count * cols_count
    split = block_out.reshape(
        local_rows, rows_count, part_rows, local_cols, cols_count, part_cols, channels
    ).transpose(1, 4, 2, 5, 0, 3, 6)
    piece = (part_rows, part_cols, local_rows * local_cols, channels)
    packed = split.reshape(devices, -1, 128)
    received = lax.all_to_all(packed, both, split_axis=0, concat_axis=0, tiled=True)
    tokens = (
        received.reshape((devices,) + piece)
        .transpose(1, 2, 0, 3, 4)
        .reshape(part_rows * part_cols, G * G, channels)
    )
    tokens = lax.optimization_barrier(tokens)
    update = attend(layer_norm(tokens, gain_grid), qkv_grid, out_grid).astype(jnp.bfloat16)
    grid_attn = (tokens.astype(jnp.float32) + update.astype(jnp.float32)).astype(jnp.bfloat16)
    grid_out = feed_forward(grid_attn, gain_gffn, ffn_in_grid, ffn_out_grid)
    grid_out = grid_out.reshape(part_rows, part_cols, devices, local_rows * local_cols, channels)
    packed = grid_out.transpose(2, 0, 1, 3, 4).reshape(devices, -1, 128)
    returned = lax.all_to_all(packed, both, split_axis=0, concat_axis=0, tiled=True)
    return (
        returned.reshape(
            rows_count, cols_count, part_rows, part_cols, local_rows, local_cols, channels
        )
        .transpose(4, 0, 2, 5, 1, 3, 6)
        .reshape(tile_rows, tile_cols, channels)
    )


def solution(mesh):
    return jax.shard_map(
        shards_body,
        mesh=mesh,
        in_specs=(
            P("rows", "cols", None),
            P(),
            P(),
            P(),
            P(),
            P(),
            P(),
            P(),
            P(),
            P(),
            P(),
            P(),
            P(),
            P(),
            P(),
            P(),
            P(),
        ),
        out_specs=P("rows", "cols", None),
        check_vma=False,
    )
```

```python
import jax
import jax.numpy as jnp
import numpy as np
from jax import lax
from jax.sharding import PartitionSpec as P

HEADS = 6
BLOCK = 8
G = 16


EPSILON = 1e-05


def layer_norm(values, scale_gain):
    values = values.astype(jnp.float32)
    average = jnp.mean(values, axis=-1, keepdims=True)
    centred = values - average
    variance = jnp.mean(centred * centred, axis=-1, keepdims=True)
    return (centred * lax.rsqrt(variance + EPSILON) * scale_gain).astype(jnp.bfloat16)


def gelu_exact(values):
    sqrt_half = np.sqrt(0.5).astype(values.dtype)
    return 0.5 * values * (1.0 + lax.erf(values * sqrt_half))


def project(normed, weight):
    flattened = normed.reshape(-1, normed.shape[-1])
    output = jnp.dot(flattened, weight, preferred_element_type=jnp.float32)
    return output.reshape(normed.shape[:-1] + (weight.shape[1],))


def attend(normed, w_qkv, w_out):
    groups, tokens, channels = normed.shape
    head_size = channels // HEADS
    w_split = w_qkv.reshape(channels, 3, HEADS, head_size)

    def heads_of(part):
        return jnp.einsum(
            "gtc,chd->ghtd", normed, w_split[:, part], preferred_element_type=jnp.float32
        ).astype(jnp.bfloat16)

    queries, keys, values = heads_of(0), heads_of(1), heads_of(2)
    scores = jnp.einsum(
        "ghtd,ghsd->ghts", queries, keys, preferred_element_type=jnp.float32
    ) * head_size ** (-0.5)
    peak = jnp.max(scores, axis=-1, keepdims=True)
    lifted = jnp.exp(scores - peak)
    total = jnp.sum(lifted, axis=-1, keepdims=True)
    weights = (lifted * (1.0 / total)).astype(jnp.bfloat16)
    mixed = jnp.einsum("ghts,ghsd->gthd", weights, values, preferred_element_type=jnp.float32)
    mixed = mixed.astype(jnp.bfloat16).reshape(groups, tokens, channels)
    return project(mixed, w_out)


def feed_forward(resid, scale_gain, w_in, w_out):
    normed = layer_norm(resid, scale_gain)
    inner_act = gelu_exact(project(normed, w_in)).astype(jnp.bfloat16)
    return (resid.astype(jnp.float32) + project(inner_act, w_out)).astype(jnp.bfloat16)


def shards_body(
    features,
    gain_conv,
    w_expand,
    w_depth,
    w_project,
    gain_block,
    qkv_block,
    out_block,
    gain_bffn,
    ffn_in_block,
    ffn_out_block,
    gain_grid,
    qkv_grid,
    out_grid,
    gain_gffn,
    ffn_in_grid,
    ffn_out_grid,
):
    rows_count = lax.axis_size("rows")
    cols_count = lax.axis_size("cols")
    tile_rows, tile_cols, channels = features.shape
    hidden_width = w_expand.shape[1]

    def expand(cells):
        return gelu_exact(project(layer_norm(cells, gain_conv), w_expand)).astype(jnp.bfloat16)

    both = ("rows", "cols")
    row_forward = [(i, i + 1) for i in range(rows_count - 1)]
    row_backward = [(t, s) for s, t in row_forward]
    col_forward = [(i, i + 1) for i in range(cols_count - 1)]
    col_backward = [(t, s) for s, t in col_forward]
    last_r, last_c = tile_rows - 1, tile_cols - 1
    top_row = lax.ppermute(features[last_r], "rows", row_forward)
    bottom_row = lax.ppermute(features[0], "rows", row_backward)
    left_source = jnp.concatenate(
        [top_row[last_c:], features[:, last_c], bottom_row[last_c:]], axis=0
    )
    right_source = jnp.concatenate([top_row[:1], features[:, 0], bottom_row[:1]], axis=0)
    left_col = lax.ppermute(left_source, "cols", col_forward)
    right_col = lax.ppermute(right_source, "cols", col_backward)
    interior_normed = layer_norm(features, gain_conv)
    interior = gelu_exact(project(interior_normed, w_expand)).astype(jnp.bfloat16)
    halo_cells = jnp.concatenate([top_row, bottom_row, left_col, right_col], axis=0)
    halo = expand(halo_cells)
    top = halo[:tile_cols][None]
    bottom = halo[tile_cols : 2 * tile_cols][None]
    left = halo[2 * tile_cols : 2 * tile_cols + tile_rows + 2][:, None]
    right = halo[2 * tile_cols + tile_rows + 2 :][:, None]
    expanded = jnp.concatenate([top, interior, bottom], axis=0)
    expanded = jnp.concatenate([left, expanded, right], axis=1)
    summed = jnp.zeros((tile_rows, tile_cols, hidden_width), jnp.float32)
    for row_tap in range(3):
        for col_tap in range(3):
            summed = summed + expanded[
                row_tap : row_tap + tile_rows, col_tap : col_tap + tile_cols
            ].astype(jnp.float32) * w_depth[row_tap, col_tap].astype(jnp.float32)
    depthwise = gelu_exact(summed).astype(jnp.bfloat16)
    conv_out = (features.astype(jnp.float32) + project(depthwise, w_project)).astype(jnp.bfloat16)
    win_rows = tile_rows // BLOCK
    win_cols = tile_cols // BLOCK
    windows = (
        conv_out.reshape(win_rows, BLOCK, win_cols, BLOCK, channels)
        .transpose(0, 2, 1, 3, 4)
        .reshape(win_rows * win_cols, BLOCK * BLOCK, channels)
    )
    windows = lax.optimization_barrier(windows)
    update = attend(layer_norm(windows, gain_block), qkv_block, out_block)
    mixed_after = (windows.astype(jnp.float32) + update).astype(jnp.bfloat16)
    mixed_after = feed_forward(mixed_after, gain_bffn, ffn_in_block, ffn_out_block)
    block_out = (
        mixed_after.reshape(win_rows, win_cols, BLOCK, BLOCK, channels)
        .transpose(0, 2, 1, 3, 4)
        .reshape(tile_rows, tile_cols, channels)
    )
    local_rows = G // rows_count
    local_cols = G // cols_count
    stride_rows = tile_rows // local_rows
    stride_cols = tile_cols // local_cols
    part_rows = stride_rows // rows_count
    part_cols = stride_cols // cols_count
    devices = rows_count * cols_count
    split = block_out.reshape(
        local_rows, rows_count, part_rows, local_cols, cols_count, part_cols, channels
    ).transpose(1, 4, 2, 5, 0, 3, 6)
    piece = (part_rows, part_cols, local_rows * local_cols, channels)
    packed = split.reshape(devices, -1, 128)
    received = lax.all_to_all(packed, both, split_axis=0, concat_axis=0, tiled=True)
    tokens = (
        received.reshape((devices,) + piece)
        .transpose(1, 2, 0, 3, 4)
        .reshape(part_rows * part_cols, G * G, channels)
    )
    tokens = lax.optimization_barrier(tokens)
    update = attend(layer_norm(tokens, gain_grid), qkv_grid, out_grid).astype(jnp.bfloat16)
    grid_attn = (tokens.astype(jnp.float32) + update.astype(jnp.float32)).astype(jnp.bfloat16)
    grid_out = feed_forward(grid_attn, gain_gffn, ffn_in_grid, ffn_out_grid)
    grid_out = grid_out.reshape(part_rows, part_cols, devices, local_rows * local_cols, channels)
    outgoing = grid_out.transpose(2, 0, 1, 3, 4)
    returned = lax.all_to_all(outgoing, both, split_axis=0, concat_axis=0, tiled=True)
    return (
        returned.reshape(
            rows_count, cols_count, part_rows, part_cols, local_rows, local_cols, channels
        )
        .transpose(4, 0, 2, 5, 1, 3, 6)
        .reshape(tile_rows, tile_cols, channels)
    )


def solution(mesh):
    return jax.shard_map(
        shards_body,
        mesh=mesh,
        in_specs=(
            P("rows", "cols", None),
            P(),
            P(),
            P(),
            P(),
            P(),
            P(),
            P(),
            P(),
            P(),
            P(),
            P(),
            P(),
            P(),
            P(),
            P(),
            P(),
        ),
        out_specs=P("rows", "cols", None),
        check_vma=False,
    )
```
